32 devices in a mesh: groups: 2 (over y), frames: 4 (over z), rows: 2 (over x), heads: 2 (over core).
Axes of the slice: x: 2, y: 2, z: 4, core: 2. Of those that a mesh axis runs over, the one named last changes fastest.
Arguments:
- queries: bfloat16 [8, 16, 64, 2240], P(('groups', 'frames'), 'rows', None, 'heads'), parts along dimension 0, may hold values from -2 to 1
- keys: bfloat16 [8, 16, 64, 2240], P(('groups', 'frames'), 'rows', None, 'heads'), parts along dimension 0, may hold values from -6 to 6
- values: bfloat16 [8, 16, 64, 2240], P(('groups', 'frames'), 'rows', None, 'heads'), parts along dimension 0, may hold values from -20 to 20
- out_weight: bfloat16 [2240, 2240], P('heads', 'frames'), may hold values from -0.125 to 0.125
Outputs:
- projected: bfloat16 [8, 16, 64, 2240], P(('groups', 'frames'), 'rows', None, 'heads'), parts along dimension 0
The draws below stay inside these ranges and needn't reach their ends.
There are 2 independent parts, one for each index of `groups`. The reference program is written for one: setup_inputs(seed, part) draws one part's arguments, and reference() takes and returns one part's arrays. A program takes and returns all parts, laid end to end along the dimension named above; an argument that names none is the same for every part. Nothing has to cross between parts.
All inputs are finite; a program needn't handle non-finite values.
Results may differ from the reference program's by a relative error of at most 0.0049.
Values may be sent and summed in bfloat16 or wider, within the bound.
A program may use at most 64 MiB of HBM per device.

```python
import jax
import jax.numpy as jnp
from jax import lax

D = 2240
HD = 112
WIDTH = 64
ROW_DEV = 8
FRAMES = 4
HEIGHT = 16


def draw_pair(key):
    base = jax.random.fold_in(key, 7)
    key_key, noise_key, shift_key = jax.random.split(base, 3)
    blocks = HEIGHT // ROW_DEV
    key_field = jnp.clip(jax.random.normal(key_key, (FRAMES, HEIGHT, WIDTH, D), jnp.float32), -6.0, 6.0)
    noise = jax.random.normal(noise_key, (FRAMES, HEIGHT, WIDTH, D), jnp.float32)
    shifts = 2.0 * jax.random.normal(shift_key, (FRAMES, blocks, 1, D), jnp.float32)
    shifts = jnp.repeat(shifts, ROW_DEV, axis=1)
    value_field = jnp.clip(3.0 * key_field + noise + shifts, -20.0, 20.0)
    return (key_field, value_field)


def draw_keys(key, part):
    return draw_pair(key)[0].astype(jnp.bfloat16)


def draw_values(key, part):
    return draw_pair(key)[1].astype(jnp.bfloat16)


def shard_levels(rng, extent, cuts, smallest, top_value):
    loudness = 1.0
    for position, parts in cuts:
        draws = jax.random.uniform(jax.random.fold_in(jax.random.fold_in(rng, 6), position), (parts,), jnp.float32, smallest / len(cuts), top_value / len(cuts))
        loudness = loudness * jnp.repeat(jnp.exp(draws), extent[position] // parts).reshape((-1,) + (1,) * (len(extent) - 1 - position))
    return loudness


def gaussian(key, shape, width, most, pieces=(), held_as=jnp.bfloat16):
    level = shard_levels(key, shape, pieces, -0.22, 0.18) if pieces else 1.0
    array = jax.random.normal(key, shape, jnp.float32) * width * level
    return jnp.minimum(jnp.maximum(array, -most), most).astype(held_as)


def setup_inputs(seed: int = 0, part: int = 0) -> dict:
    key_of = jax.random.split(jax.random.key(seed), 5)
    own_keys = jax.random.split(jax.random.fold_in(key_of[4], part), 5)
    return {
        "queries": jnp.clip(-2.0 + 3.0 * jax.random.uniform(own_keys[0], (FRAMES, HEIGHT, WIDTH, D), jnp.float32) ** shard_levels(own_keys[0], (FRAMES, HEIGHT, WIDTH, D), ((0, 4), (1, 2), (3, 2)), -0.2, 0.2), -2.0, 1.0).astype(jnp.bfloat16),
        "keys": draw_keys(jax.random.fold_in(jax.random.fold_in(key_of[4], part), 71), part),
        "values": draw_values(jax.random.fold_in(jax.random.fold_in(key_of[4], part), 71), part),
        "out_weight": gaussian(key_of[3], (D, D), D ** -0.5, 0.125, ((0, 2), (1, 4))),
    }


EPS = 1e-6


def reference(queries, keys, values, out_weight):
    frames_all, height_all, width_all, features = queries.shape
    heads = features // HD
    shape4 = (frames_all, height_all * width_all, heads, HD)
    query_pos = jnp.maximum(queries, 0).reshape(shape4).astype(jnp.float32)
    key_pos = jnp.maximum(keys, 0).reshape(shape4).astype(jnp.float32)
    value_rows = values.reshape(shape4).astype(jnp.float32)
    frame_state = jnp.einsum("fthd,fthe->fhde", key_pos, value_rows, precision=lax.Precision.HIGHEST)
    frame_norm = jnp.sum(key_pos, axis=1)
    state = jnp.cumsum(frame_state, axis=0)
    norm = jnp.cumsum(frame_norm, axis=0)
    numer = jnp.einsum("fthd,fhde->fthe", query_pos, state, precision=lax.Precision.HIGHEST)
    denom = jnp.einsum("fthd,fhd->fth", query_pos, norm, precision=lax.Precision.HIGHEST)
    attended = (numer / (denom[..., None] + EPS)).astype(jnp.bfloat16)
    attended = attended.reshape(frames_all * height_all * width_all, features)
    projected = jnp.dot(attended, out_weight, preferred_element_type=jnp.float32).astype(jnp.bfloat16)
    return projected.reshape(frames_all, height_all, width_all, features)
```

```python
import functools

import jax
import jax.numpy as jnp
from jax import lax
from jax.experimental import pallas as pl
from jax.experimental.pallas import tpu as pltpu
from jax.sharding import PartitionSpec as P

HD = 112
EPS = 1e-06
LANES = 128
MESH = pl.DeviceIdType.MESH


def prefix_before(local):
    position = lax.axis_index("frames") * local[0].shape[0]
    pieces = (
        lax.all_gather(local[0], "frames", axis=0, tiled=True),
        lax.all_gather(local[1], "frames", axis=0, tiled=True),
    )
    count = pieces[0].shape[0]
    keep = jnp.arange(count, dtype=jnp.int32) < position
    states = jnp.sum(jnp.where(keep[:, None, None, None], pieces[0], 0.0), axis=0, keepdims=True)
    totals = jnp.sum(jnp.where(keep[:, None, None], pieces[1], 0.0), axis=0, keepdims=True)
    return (states, totals)


def general(queries, keys, values, out_weight):
    frames_here, rows_here, columns, features = queries.shape
    heads_here = features // HD
    shape4 = (frames_here, rows_here * columns, heads_here, HD)
    query_pos = jnp.maximum(queries, 0).reshape(shape4).astype(jnp.float32)
    key_pos = jnp.maximum(keys, 0).reshape(shape4)
    value_rows = values.reshape(shape4)
    frame_state = jnp.einsum(
        "fthd,fthe->fhde", key_pos, value_rows, preferred_element_type=jnp.float32
    )
    frame_norm = jnp.sum(key_pos.astype(jnp.float32), axis=1)
    own = lax.psum((frame_state, frame_norm), "rows")
    earlier = prefix_before(own)
    state = own[0] + earlier[0]
    norm = own[1] + earlier[1]
    numer = jnp.einsum("fthd,fhde->fthe", query_pos, state, precision=lax.Precision.HIGHEST)
    denom = jnp.einsum("fthd,fhd->fth", query_pos, norm, precision=lax.Precision.HIGHEST)
    attended = (numer / (denom[..., None] + EPS)).astype(jnp.bfloat16)
    attended = attended.reshape(frames_here * rows_here * columns, features)
    terms = jnp.dot(
        attended,
        lax.all_gather(out_weight, "frames", axis=1, tiled=True),
        preferred_element_type=jnp.float32,
    )
    mixed = lax.psum_scatter(terms, "heads", scatter_dimension=1, tiled=True).astype(jnp.bfloat16)
    return mixed.reshape(frames_here, rows_here, columns, mixed.shape[1])


A, D, X, Y = 0, 1, 2, 3


def kernel(
    nz, q_ref, k_ref, v_ref, w_ref, out_ref,
    wbuf, att, st, own5, rs_send, rs_recv, z_send, z_recv, fin,
    w_recv, own_send, rel_send, block_sem, rs_sem, zs_send, zs_recv, ag_sem, at_send, at_recv,
):
    y, z = lax.axis_index("groups"), lax.axis_index("frames")
    x, c = lax.axis_index("rows"), lax.axis_index("heads")
    heads, _, wide = w_ref.shape
    tokens = q_ref.shape[0]
    half = heads // 2
    slots = nz // 2
    via_x = half * 2 // 5
    home = z // slots

    def dev(x_=None, y_=None, z_=None, c_=None):
        return (
            y if y_ is None else y_,
            z if z_ is None else z_,
            x if x_ is None else x_,
            c if c_ is None else c_,
        )

    x_nb, y_nb, partner = dev(x_=1 - x), dev(y_=1 - y), dev(c_=1 - c)

    barrier = pltpu.get_barrier_semaphore()
    greeted = [x_nb, y_nb, partner]
    for step in range(1, nz):
        for core in range(2):
            greeted.append(dev(z_=lax.rem(z + step, nz), c_=core))
    for device in greeted:
        pl.semaphore_signal(barrier, inc=1, device_id=device, device_id_type=MESH)
    pl.semaphore_wait(barrier, len(greeted))

    def remote(src, dst, send, recv, device):
        return pltpu.make_async_remote_copy(
            src_ref=src, dst_ref=dst, send_sem=send, recv_sem=recv,
            device_id=device, device_id_type=MESH,
        )

    mine = lax.rem(x + y + c, 2)
    kind = jnp.where(c == x, A, D)

    def own_copy(side, j):
        target = z + 1 - 2 * side
        head = mine * half + j
        return remote(
            w_ref.at[head],
            wbuf.at[lax.rem(z, slots), c * heads + head, pl.ds(0, HD)],
            own_send.at[side, j],
            w_recv.at[lax.rem(z, slots), kind, j],
            dev(z_=target, c_=home),
        )

    def own_each(act):
        for side in range(2):
            @pl.when((z < nz - 1) if side == 0 else (z > 0))
            def _():
                def body(j, carry):
                    act(own_copy(side, j))
                    return carry
                lax.fori_loop(0, half, body, 0)

    @pl.when(c == x)
    def _():
        own_each(lambda copy: copy.start())

    block_dst = wbuf.at[lax.rem(z, slots), pl.ds(c * heads, heads), pl.ds(0, HD)]
    block_local = pltpu.make_async_copy(w_ref, block_dst, block_sem.at[0])
    block_out = remote(w_ref, block_dst, block_sem.at[1], block_sem.at[2], partner)

    @pl.when(home == c)
    def _():
        block_local.start()

    @pl.when(home != c)
    def _():
        block_out.start()

    wbuf[:, :, HD:, :] = jnp.zeros((slots, 2 * heads, LANES - HD, wide), wbuf.dtype)

    base = {
        A: x * heads + y * half,
        D: (1 - x) * heads + (1 - y) * half,
        X: (1 - x) * heads + y * half,
        Y: x * heads + (1 - y) * half,
    }

    def slot(i):
        s = jnp.where(z <= slots * c, i, slots - 1 - i)
        source = slots * c + s
        return s, source, jnp.abs(source - z)

    def relay(s, what, j, lane, to_kind, device):
        ref = wbuf.at[s, base[what] + j, pl.ds(0, HD)]
        return remote(ref, ref, rel_send.at[s, lane, j], w_recv.at[s, to_kind, j], device)

    def arrived(s, what, j):
        ref = wbuf.at[s, base[what] + j, pl.ds(0, HD)]
        remote(ref, ref, rel_send.at[s, 0, j], w_recv.at[s, what, j], x_nb).wait_recv()

    def relays_a(s, source, j):
        onward = jnp.where(source < z, z + 1, z - 1)
        target = jnp.clip(onward, 0, nz - 1)
        return (
            ((onward >= 0) & (onward < nz), relay(s, A, j, 2, A, dev(z_=target))),
            (None, relay(s, A, j, 0, X, x_nb)),
            (None, relay(s, A, j, 1, Y, y_nb)),
        )

    def on_a(i, wanted):
        s, source, far = slot(i)

        @pl.when(wanted(far))
        def _():
            def body(j, carry):
                arrived(s, A, j)
                for needed, copy in relays_a(s, source, j):
                    if needed is None:
                        copy.start()
                    else:
                        @pl.when(needed)
                        def _():
                            copy.start()
                return carry
            lax.fori_loop(0, half, body, 0)

    def on_xy(i):
        s, source, far = slot(i)

        @pl.when(far > 0)
        def _():
            def first(j, carry):
                arrived(s, X, j)
                arrived(s, Y, j)

                @pl.when(far > 1)
                def _():
                    relay(s, Y, j, 3, D, x_nb).start()
                return carry

            def second(j, carry):
                arrived(s, X, j)
                arrived(s, Y, j)

                @pl.when(far > 1)
                def _():
                    relay(s, X, j, 3, D, y_nb).start()
                return carry
            lax.fori_loop(0, via_x, first, 0)
            lax.fori_loop(via_x, half, second, 0)

    def on_d(i):
        s, source, far = slot(i)

        @pl.when(far > 0)
        def _():
            def body(j, carry):
                arrived(s, D, j)
                return carry
            lax.fori_loop(0, half, body, 0)

        @pl.when(far == 0)
        def _():
            block_local.wait()
            other = wbuf.at[lax.rem(z, slots), pl.ds((1 - c) * heads, heads), pl.ds(0, HD)]
            remote(w_ref, other, block_sem.at[1], block_sem.at[2], partner).wait_recv()

    def drain(i):
        s, source, far = slot(i)

        @pl.when(far > 0)
        def _():
            def body(j, carry):
                for needed, copy in relays_a(s, source, j):
                    if needed is None:
                        copy.wait_send()
                    else:
                        @pl.when(needed)
                        def _():
                            copy.wait_send()

                @pl.when(far > 1)
                def _():
                    relay(s, X, j, 3, D, y_nb).wait_send()
                return carry
            lax.fori_loop(0, half, body, 0)

    ones = jnp.ones((tokens, LANES), jnp.bfloat16)
    for h in range(heads):
        cols = slice(h * HD, (h + 1) * HD)
        kp = jnp.maximum(k_ref[:, cols], 0)
        dims = (((0,), (0,)), ((), ()))
        st[h, :, :HD] = lax.dot_general(
            kp, v_ref[:, cols], dims, preferred_element_type=jnp.float32)
        total = lax.dot_general(kp, ones, dims, preferred_element_type=jnp.float32)
        st[h, :, HD:] = total[:, HD:]

    rs_send[...] = st[pl.ds((1 - x) * half, half)].astype(jnp.bfloat16)
    rs = remote(rs_send, rs_recv, rs_sem.at[0], rs_sem.at[1], x_nb)
    rs.start()
    for i in range(slots):
        on_a(i, lambda far: far == 1)
    rs.wait_recv()
    own5[...] = st[pl.ds(x * half, half)] + rs_recv[...].astype(jnp.float32)
    z_send[...] = own5[...].astype(jnp.bfloat16)

    def state_copy(step):
        target = jnp.minimum(z + step, nz - 1)
        return remote(z_send, z_recv.at[step - 1], zs_send.at[step - 1], zs_recv.at[step - 1],
                      dev(z_=target))

    for step in range(1, nz):
        @pl.when(z + step < nz)
        def _():
            state_copy(step).start()

    @pl.when(c != x)
    def _():
        own_each(lambda copy: copy.start())

    on_a(0, lambda far: far > 1)
    for step in range(1, nz):
        @pl.when(z >= step)
        def _():
            state_copy(step).wait_recv()
            own5[...] += z_recv[step - 1].astype(jnp.float32)

    fin[pl.ds(x * half, half)] = own5[...].astype(jnp.bfloat16)
    ag = remote(fin.at[pl.ds(x * half, half)], fin.at[pl.ds(x * half, half)],
                ag_sem.at[0], ag_sem.at[1], x_nb)
    ag.start()
    on_xy(0)
    for i in range(1, slots):
        on_a(i, lambda far: far > 1)
    other5 = fin.at[pl.ds((1 - x) * half, half)]
    remote(other5, other5, ag_sem.at[0], ag_sem.at[1], x_nb).wait_recv()

    lane = lax.broadcasted_iota(jnp.int32, (tokens, LANES), 1)

    def att_copy(h):
        ref = att.at[c, :, pl.ds(h * LANES, LANES)]
        return remote(ref, ref, at_send.at[h], at_recv.at[h], partner)

    for h in range(heads):
        qp = jnp.maximum(q_ref[:, h * HD:(h + 1) * HD], 0)
        both = jnp.dot(qp, fin[h], preferred_element_type=jnp.float32)
        share = jnp.where(lane < HD, both / (both[:, HD:HD + 1] + EPS), 0.0)
        att[c, :, h * LANES:(h + 1) * LANES] = share.astype(jnp.bfloat16)
        att_copy(h).start()
    for h in range(heads):
        ref = att.at[1 - c, :, pl.ds(h * LANES, LANES)]
        remote(ref, ref, at_send.at[h], at_recv.at[h], partner).wait_recv()

    for i in range(slots):
        s = slot(i)[0]
        if i:
            on_xy(i)
        on_d(i)
        out = None
        for r in range(2):
            part = jnp.dot(
                att[r],
                wbuf[s, r * heads:(r + 1) * heads].reshape(heads * LANES, wide),
                preferred_element_type=jnp.float32,
            )
            out = part if out is None else out + part
        out = out.astype(out_ref.dtype)
        for place in range(slots):
            @pl.when(s == place)
            def _():
                out_ref[:, place * wide:(place + 1) * wide] = out

    own_each(lambda copy: copy.wait_send())

    @pl.when(home != c)
    def _():
        block_out.wait_send()
    rs.wait_send()
    for step in range(1, nz):
        @pl.when(z + step < nz)
        def _():
            state_copy(step).wait_send()
    ag.wait_send()
    for h in range(heads):
        att_copy(h).wait_send()
    for i in range(slots):
        drain(i)


def fused(nz, queries, keys, values, out_weight):
    frames_here, rows_here, columns, features = queries.shape
    tokens = frames_here * rows_here * columns
    heads, half, wide = features // HD, features // HD // 2, out_weight.shape[1]
    slots = nz // 2
    state = (half, HD, LANES)
    vmem = pl.BlockSpec(memory_space=pltpu.VMEM)
    bf16, f32 = jnp.bfloat16, jnp.float32
    dma = pltpu.SemaphoreType.DMA
    out = pl.pallas_call(
        functools.partial(kernel, nz),
        out_shape=jax.ShapeDtypeStruct((tokens, slots * wide), bf16),
        in_specs=[vmem, vmem, vmem, pl.BlockSpec(memory_space=pl.ANY)],
        out_specs=vmem,
        scratch_shapes=[
            pltpu.VMEM((slots, 2 * heads, LANES, wide), bf16),
            pltpu.VMEM((2, tokens, heads * LANES), bf16),
            pltpu.VMEM((heads, HD, LANES), f32),
            pltpu.VMEM(state, f32),
            pltpu.VMEM(state, bf16),
            pltpu.VMEM(state, bf16),
            pltpu.VMEM(state, bf16),
            pltpu.VMEM((nz - 1,) + state, bf16),
            pltpu.VMEM((heads, HD, LANES), bf16),
            dma((slots, 4, half)),
            dma((2, half)),
            dma((slots, 4, half)),
            dma((3,)),
            dma((2,)),
            dma((nz - 1,)),
            dma((nz - 1,)),
            dma((2,)),
            dma((heads,)),
            dma((heads,)),
        ],
        compiler_params=pltpu.CompilerParams(
            collective_id=0, has_side_effects=True, vmem_limit_bytes=56 * 2**20),
        name="attend_project",
    )(
        queries.reshape(tokens, features),
        keys.reshape(tokens, features),
        values.reshape(tokens, features),
        out_weight.reshape(heads, HD, wide),
    )
    return out.reshape(frames_here, rows_here, columns, slots * wide)


def solution(mesh):
    size = dict(mesh.shape)
    pairs = size["rows"] == 2 and size["groups"] == 2 and size["heads"] == 2
    body = general
    if pairs and size["frames"] == 4:
        body = functools.partial(fused, size["frames"])
    return jax.shard_map(
        body,
        mesh=mesh,
        in_specs=(
            P(("groups", "frames"), "rows", None, "heads"),
            P(("groups", "frames"), "rows", None, "heads"),
            P(("groups", "frames"), "rows", None, "heads"),
            P("heads", "frames"),
        ),
        out_specs=P(("groups", "frames"), "rows", None, "heads"),
        check_vma=False,
    )
```

```python
import functools

import jax
import jax.numpy as jnp
from jax import lax
from jax.experimental import pallas as pl
from jax.experimental.pallas import tpu as pltpu
from jax.sharding import PartitionSpec as P

HD = 112
EPS = 1e-06
LANES = 128
MESH = pl.DeviceIdType.MESH


def prefix_before(local):
    position = lax.axis_index("frames") * local[0].shape[0]
    pieces = (
        lax.all_gather(local[0], "frames", axis=0, tiled=True),
        lax.all_gather(local[1], "frames", axis=0, tiled=True),
    )
    count = pieces[0].shape[0]
    keep = jnp.arange(count, dtype=jnp.int32) < position
    states = jnp.sum(jnp.where(keep[:, None, None, None], pieces[0], 0.0), axis=0, keepdims=True)
    totals = jnp.sum(jnp.where(keep[:, None, None], pieces[1], 0.0), axis=0, keepdims=True)
    return (states, totals)


def general(queries, keys, values, out_weight):
    frames_here, rows_here, columns, features = queries.shape
    heads_here = features // HD
    shape4 = (frames_here, rows_here * columns, heads_here, HD)
    query_pos = jnp.maximum(queries, 0).reshape(shape4).astype(jnp.float32)
    key_pos = jnp.maximum(keys, 0).reshape(shape4)
    value_rows = values.reshape(shape4)
    frame_state = jnp.einsum(
        "fthd,fthe->fhde", key_pos, value_rows, preferred_element_type=jnp.float32
    )
    frame_norm = jnp.sum(key_pos.astype(jnp.float32), axis=1)
    own = lax.psum((frame_state, frame_norm), "rows")
    earlier = prefix_before(own)
    state = own[0] + earlier[0]
    norm = own[1] + earlier[1]
    numer = jnp.einsum("fthd,fhde->fthe", query_pos, state, precision=lax.Precision.HIGHEST)
    denom = jnp.einsum("fthd,fhd->fth", query_pos, norm, precision=lax.Precision.HIGHEST)
    attended = (numer / (denom[..., None] + EPS)).astype(jnp.bfloat16)
    attended = attended.reshape(frames_here * rows_here * columns, features)
    terms = jnp.dot(
        attended,
        lax.all_gather(out_weight, "frames", axis=1, tiled=True),
        preferred_element_type=jnp.float32,
    )
    mixed = lax.psum_scatter(terms, "heads", scatter_dimension=1, tiled=True).astype(jnp.bfloat16)
    return mixed.reshape(frames_here, rows_here, columns, mixed.shape[1])


A, D, X, Y = 0, 1, 2, 3
PIECES = 5


def kernel(
    nz, q_hbm, k_hbm, v_hbm, w_ref, out_ref,
    q_ref, k_ref, v_ref, wbuf, att, st, own5, rs_send, rs_recv, z_recv, fin,
    in_sem, w_recv, own_send, rel_send, block_sem, rs_out, rs_in, z_out, z_in, ag_out, ag_in, at_sem,
):
    y, z = lax.axis_index("groups"), lax.axis_index("frames")
    x, c = lax.axis_index("rows"), lax.axis_index("heads")
    chunks = w_ref.shape[0]
    tokens, features = q_ref.shape
    wide = w_ref.shape[0] * w_ref.shape[1]
    heads = features // HD
    half = heads // 2
    parts = chunks // 2
    slots = nz // 2
    home = z // slots
    spot = lax.rem(z, slots)

    def dev(x_=None, y_=None, z_=None, c_=None):
        return (
            y if y_ is None else y_,
            z if z_ is None else z_,
            x if x_ is None else x_,
            c if c_ is None else c_,
        )

    x_nb, y_nb, partner = dev(x_=1 - x), dev(y_=1 - y), dev(c_=1 - c)

    loads = [
        pltpu.make_async_copy(src, dst, in_sem.at[n])
        for n, (src, dst) in enumerate(((k_hbm, k_ref), (v_hbm, v_ref), (q_hbm, q_ref)))
    ]
    for load in loads:
        load.start()

    barrier = pltpu.get_barrier_semaphore()
    greeted = [x_nb, y_nb, partner]
    for step in range(1, nz):
        for core in range(2):
            greeted.append(dev(z_=lax.rem(z + step, nz), c_=core))
    for device in greeted:
        pl.semaphore_signal(barrier, inc=1, device_id=device, device_id_type=MESH)
    pl.semaphore_wait(barrier, len(greeted))

    def remote(src, dst, send, recv, device):
        return pltpu.make_async_remote_copy(
            src_ref=src, dst_ref=dst, send_sem=send, recv_sem=recv,
            device_id=device, device_id_type=MESH,
        )

    def each(count, act, begin=0):
        def body(j, carry):
            act(j)
            return carry
        lax.fori_loop(begin, count, body, 0)

    mine = lax.rem(x + y + c, 2)
    kind = jnp.where(c == x, A, D)

    def own_copy(side, j):
        chunk = mine * parts + j
        return remote(
            w_ref.at[chunk],
            wbuf.at[spot, c, chunk],
            own_send.at[side, j],
            w_recv.at[spot, kind, j],
            dev(z_=z + 1 - 2 * side, c_=home),
        )

    def own_each(act):
        for side in range(2):
            @pl.when((z < nz - 1) if side == 0 else (z > 0))
            def _():
                each(parts, lambda j: act(own_copy(side, j)))

    @pl.when(c == x)
    def _():
        own_each(lambda copy: copy.start())

    block_local = pltpu.make_async_copy(w_ref, wbuf.at[spot, c], block_sem.at[0])
    block_out = remote(w_ref, wbuf.at[spot, c], block_sem.at[1], block_sem.at[2], partner)

    @pl.when(home == c)
    def _():
        block_local.start()

    @pl.when(home != c)
    def _():
        block_out.start()

    base = {A: (x, y * parts), D: (1 - x, (1 - y) * parts),
            X: (1 - x, y * parts), Y: (x, (1 - y) * parts)}

    def slot(i):
        s = jnp.where(z <= slots * c, i, slots - 1 - i)
        source = slots * c + s
        return s, source, jnp.abs(source - z)

    def relay(s, what, j, lane, to_kind, device):
        rows, first = base[what]
        ref = wbuf.at[s, rows, first + j]
        return remote(ref, ref, rel_send.at[s, lane, j], w_recv.at[s, to_kind, j], device)

    def arrived(s, what, j):
        relay(s, what, j, 0, what, x_nb).wait_recv()

    def relays_a(s, source, j):
        onward = jnp.where(source < z, z + 1, z - 1)
        return (
            ((onward >= 0) & (onward < nz),
             relay(s, A, j, 2, A, dev(z_=jnp.clip(onward, 0, nz - 1)))),
            (None, relay(s, A, j, 0, X, x_nb)),
            (None, relay(s, A, j, 1, Y, y_nb)),
        )

    def on_a(i, wanted, j):
        s, source, far = slot(i)

        @pl.when(wanted(far))
        def _():
            arrived(s, A, j)
            for needed, copy in relays_a(s, source, j):
                if needed is None:
                    copy.start()
                else:
                    @pl.when(needed)
                    def _():
                        copy.start()

    def by_x(far):
        return jnp.where(far == 2, (2 * parts) // PIECES, parts // PIECES)

    def on_xy(i, wanted, j):
        s, source, far = slot(i)

        @pl.when(wanted(far))
        def _():
            arrived(s, X, j)
            arrived(s, Y, j)

            @pl.when((far > 1) & (j < by_x(far)))
            def _():
                relay(s, Y, j, 3, D, x_nb).start()

            @pl.when((far > 1) & (j >= by_x(far)))
            def _():
                relay(s, X, j, 3, D, y_nb).start()

    def on_d(i):
        s, source, far = slot(i)

        @pl.when(far > 0)
        def _():
            each(parts, lambda j: arrived(s, D, j))

        @pl.when(far == 0)
        def _():
            block_local.wait()
            other = wbuf.at[spot, 1 - c]
            remote(w_ref, other, block_sem.at[1], block_sem.at[2], partner).wait_recv()

    def drain(i):
        s, source, far = slot(i)

        def one(j):
            for needed, copy in relays_a(s, source, j):
                if needed is None:
                    copy.wait_send()
                else:
                    @pl.when(needed)
                    def _():
                        copy.wait_send()

            @pl.when(far > 1)
            def _():
                relay(s, X, j, 3, D, y_nb).wait_send()

        @pl.when(far > 0)
        def _():
            each(parts, one)

    def rs(j):
        return remote(rs_send.at[j], rs_recv.at[j], rs_out.at[j], rs_in.at[j], x_nb)

    loads[0].wait()
    loads[1].wait()
    ones = jnp.ones((tokens, LANES), jnp.bfloat16)
    for j in range(half):
        for h in (j, half + j):
            cols = slice(h * HD, (h + 1) * HD)
            kp = jnp.maximum(k_ref[:, cols], 0)
            dims = (((0,), (0,)), ((), ()))
            st[h, :, :HD] = lax.dot_general(
                kp, v_ref[:, cols], dims, preferred_element_type=jnp.float32)
            total = lax.dot_general(kp, ones, dims, preferred_element_type=jnp.float32)
            st[h, :, HD:] = total[:, HD:]
        rs_send[j] = st[(1 - x) * half + j].astype(jnp.bfloat16)
        rs(j).start()

    def up(j):
        return remote(fin.at[x * half + j], z_recv.at[j], z_out.at[j], z_in.at[j],
                      dev(z_=jnp.minimum(z + 1, nz - 1)))

    def across(j):
        ref = fin.at[x * half + j]
        return remote(ref, ref, ag_out.at[j], ag_in.at[j], x_nb)

    def finish(j, total):
        fin[x * half + j] = total.astype(jnp.bfloat16)

        @pl.when(z < nz - 1)
        def _():
            up(j).start()
        across(j).start()

    def near_step(j):
        for i in range(slots):
            on_a(i, lambda far: far == 1, j)
        rs(j).wait_recv()
        total = st[x * half + j] + rs_recv[j].astype(jnp.float32)
        own5[j] = total

        @pl.when(z == 0)
        def _():
            finish(j, total)

    def next_step(j):
        @pl.when(z > 0)
        def _():
            up(j).wait_recv()
            finish(j, own5[j] + z_recv[j].astype(jnp.float32))
        for i in range(slots):
            on_a(i, lambda far: far == 2, j)

    def far_step(j):
        for i in range(slots):
            on_a(i, lambda far: far > 2, j)
        for i in range(slots):
            on_xy(i, lambda far: far == 2, j)

    each(half, near_step)
    each(half, next_step)

    @pl.when(c != x)
    def _():
        own_each(lambda copy: copy.start())

    each(parts, far_step)

    def across_in(j):
        ref = fin.at[(1 - x) * half + j]
        remote(ref, ref, ag_out.at[j], ag_in.at[j], x_nb).wait_recv()

    each(half, across_in)

    loads[2].wait()
    for h in range(heads):
        qp = jnp.maximum(q_ref[:, h * HD:(h + 1) * HD], 0)
        both = jnp.dot(qp, fin[h], preferred_element_type=jnp.float32)
        share = both[:, :HD] / (both[:, HD:HD + 1] + EPS)
        att[c, :, h * HD:(h + 1) * HD] = share.astype(jnp.bfloat16)
    att_out = remote(att.at[c], att.at[c], at_sem.at[0], at_sem.at[1], partner)
    att_out.start()
    each(parts, lambda j: [on_xy(i, lambda far: (far == 1) | (far > 2), j) for i in range(slots)] and None)
    remote(att.at[1 - c], att.at[1 - c], at_sem.at[0], at_sem.at[1], partner).wait_recv()

    for i in range(slots):
        s = slot(i)[0]
        on_d(i)
        out = None
        for r in range(2):
            part = lax.dot_general(
                att[r], wbuf[s, r].reshape(wide, features),
                (((1,), (1,)), ((), ())), preferred_element_type=jnp.float32,
            )
            out = part if out is None else out + part
        out = out.astype(out_ref.dtype)
        for place in range(slots):
            @pl.when(s == place)
            def _():
                out_ref[:, place * wide:(place + 1) * wide] = out

    own_each(lambda copy: copy.wait_send())

    @pl.when(home != c)
    def _():
        block_out.wait_send()

    def sent(j):
        rs(j).wait_send()
        across(j).wait_send()

        @pl.when(z < nz - 1)
        def _():
            up(j).wait_send()

    each(half, sent)
    att_out.wait_send()
    for i in range(slots):
        drain(i)


def fused(nz, queries, keys, values, out_weight):
    frames_here, rows_here, columns, features = queries.shape
    tokens = frames_here * rows_here * columns
    heads, half, wide = features // HD, features // HD // 2, out_weight.shape[1]
    slots = nz // 2
    chunks = 2 * PIECES
    parts = PIECES
    width = wide // chunks
    vmem, hbm = pl.BlockSpec(memory_space=pltpu.VMEM), pl.BlockSpec(memory_space=pl.ANY)
    bf16, f32 = jnp.bfloat16, jnp.float32
    dma = pltpu.SemaphoreType.DMA
    out = pl.pallas_call(
        functools.partial(kernel, nz),
        out_shape=jax.ShapeDtypeStruct((tokens, slots * wide), bf16),
        in_specs=[hbm] * 4,
        out_specs=vmem,
        scratch_shapes=[
            pltpu.VMEM((tokens, features), bf16),
            pltpu.VMEM((tokens, features), bf16),
            pltpu.VMEM((tokens, features), bf16),
            pltpu.VMEM((slots, 2, chunks, width, features), bf16),
            pltpu.VMEM((2, tokens, features), bf16),
            pltpu.VMEM((heads, HD, LANES), f32),
            pltpu.VMEM((half, HD, LANES), f32),
            pltpu.VMEM((half, HD, LANES), bf16),
            pltpu.VMEM((half, HD, LANES), bf16),
            pltpu.VMEM((half, HD, LANES), bf16),
            pltpu.VMEM((heads, HD, LANES), bf16),
            dma((3,)),
            dma((slots, 4, parts)),
            dma((2, parts)),
            dma((slots, 4, parts)),
            dma((3,)),
            dma((half,)),
            dma((half,)),
            dma((half,)),
            dma((half,)),
            dma((half,)),
            dma((half,)),
            dma((2,)),
        ],
        compiler_params=pltpu.CompilerParams(
            collective_id=0, has_side_effects=True, vmem_limit_bytes=56 * 2**20),
        name="attend_project",
    )(
        queries.reshape(tokens, features),
        keys.reshape(tokens, features),
        values.reshape(tokens, features),
        out_weight.T.reshape(chunks, width, features),
    )
    return out.reshape(frames_here, rows_here, columns, slots * wide)


def solution(mesh):
    size = dict(mesh.shape)
    pairs = size["rows"] == 2 and size["groups"] == 2 and size["heads"] == 2
    body = general
    if pairs and size["frames"] == 4:
        body = functools.partial(fused, size["frames"])
    return jax.shard_map(
        body,
        mesh=mesh,
        in_specs=(
            P(("groups", "frames"), "rows", None, "heads"),
            P(("groups", "frames"), "rows", None, "heads"),
            P(("groups", "frames"), "rows", None, "heads"),
            P("heads", "frames"),
        ),
        out_specs=P(("groups", "frames"), "rows", None, "heads"),
        check_vma=False,
    )
```

```python
import functools

import jax
import jax.numpy as jnp
from jax import lax
from jax.experimental import pallas as pl
from jax.experimental.pallas import tpu as pltpu
from jax.sharding import PartitionSpec as P

HD = 112
EPS = 1e-06
LANES = 128
MESH = pl.DeviceIdType.MESH


def prefix_before(local):
    position = lax.axis_index("frames") * local[0].shape[0]
    pieces = (
        lax.all_gather(local[0], "frames", axis=0, tiled=True),
        lax.all_gather(local[1], "frames", axis=0, tiled=True),
    )
    count = pieces[0].shape[0]
    keep = jnp.arange(count, dtype=jnp.int32) < position
    states = jnp.sum(jnp.where(keep[:, None, None, None], pieces[0], 0.0), axis=0, keepdims=True)
    totals = jnp.sum(jnp.where(keep[:, None, None], pieces[1], 0.0), axis=0, keepdims=True)
    return (states, totals)


def general(queries, keys, values, out_weight):
    frames_here, rows_here, columns, features = queries.shape
    heads_here = features // HD
    shape4 = (frames_here, rows_here * columns, heads_here, HD)
    query_pos = jnp.maximum(queries, 0).reshape(shape4).astype(jnp.float32)
    key_pos = jnp.maximum(keys, 0).reshape(shape4)
    value_rows = values.reshape(shape4)
    frame_state = jnp.einsum(
        "fthd,fthe->fhde", key_pos, value_rows, preferred_element_type=jnp.float32
    )
    frame_norm = jnp.sum(key_pos.astype(jnp.float32), axis=1)
    own = lax.psum((frame_state, frame_norm), "rows")
    earlier = prefix_before(own)
    state = own[0] + earlier[0]
    norm = own[1] + earlier[1]
    numer = jnp.einsum("fthd,fhde->fthe", query_pos, state, precision=lax.Precision.HIGHEST)
    denom = jnp.einsum("fthd,fhd->fth", query_pos, norm, precision=lax.Precision.HIGHEST)
    attended = (numer / (denom[..., None] + EPS)).astype(jnp.bfloat16)
    attended = attended.reshape(frames_here * rows_here * columns, features)
    terms = jnp.dot(
        attended,
        lax.all_gather(out_weight, "frames", axis=1, tiled=True),
        preferred_element_type=jnp.float32,
    )
    mixed = lax.psum_scatter(terms, "heads", scatter_dimension=1, tiled=True).astype(jnp.bfloat16)
    return mixed.reshape(frames_here, rows_here, columns, mixed.shape[1])


A, D, X, Y = 0, 1, 2, 3
PIECES = 5


def kernel(
    nz, q_hbm, k_hbm, v_hbm, w_ref, out_ref,
    q_ref, k_ref, v_ref, wbuf, att, st, own5, rs_send, rs_recv, z_recv, fin,
    in_sem, w_recv, own_send, rel_send, block_sem, rs_out, rs_in, z_out, z_in, ag_out, ag_in, at_sem,
):
    y, z = lax.axis_index("groups"), lax.axis_index("frames")
    x, c = lax.axis_index("rows"), lax.axis_index("heads")
    chunks = w_ref.shape[0]
    tokens, features = q_ref.shape
    wide = w_ref.shape[0] * w_ref.shape[1]
    heads = features // HD
    half = heads // 2
    parts = chunks // 2
    slots = nz // 2
    home = z // slots
    spot = lax.rem(z, slots)

    def dev(x_=None, y_=None, z_=None, c_=None):
        return (
            y if y_ is None else y_,
            z if z_ is None else z_,
            x if x_ is None else x_,
            c if c_ is None else c_,
        )

    x_nb, y_nb, partner = dev(x_=1 - x), dev(y_=1 - y), dev(c_=1 - c)

    loads = [
        pltpu.make_async_copy(src, dst, in_sem.at[n])
        for n, (src, dst) in enumerate(((k_hbm, k_ref), (v_hbm, v_ref), (q_hbm, q_ref)))
    ]
    for load in loads:
        load.start()

    barrier = pltpu.get_barrier_semaphore()
    greeted = [x_nb, y_nb, partner]
    for step in range(1, nz):
        for core in range(2):
            greeted.append(dev(z_=lax.rem(z + step, nz), c_=core))
    for device in greeted:
        pl.semaphore_signal(barrier, inc=1, device_id=device, device_id_type=MESH)
    pl.semaphore_wait(barrier, len(greeted))

    def remote(src, dst, send, recv, device):
        return pltpu.make_async_remote_copy(
            src_ref=src, dst_ref=dst, send_sem=send, recv_sem=recv,
            device_id=device, device_id_type=MESH,
        )

    def each(count, act, begin=0):
        def body(j, carry):
            act(j)
            return carry
        lax.fori_loop(begin, count, body, 0)

    mine = lax.rem(x + y + c, 2)
    kind = jnp.where(c == x, A, D)

    def own_copy(side, j):
        chunk = mine * parts + j
        return remote(
            w_ref.at[chunk],
            wbuf.at[spot, c, chunk],
            own_send.at[side, j],
            w_recv.at[spot, kind, j],
            dev(z_=z + 1 - 2 * side, c_=home),
        )

    def own_each(act):
        for side in range(2):
            @pl.when((z < nz - 1) if side == 0 else (z > 0))
            def _():
                each(parts, lambda j: act(own_copy(side, j)))

    @pl.when(c == x)
    def _():
        own_each(lambda copy: copy.start())

    block_local = pltpu.make_async_copy(w_ref, wbuf.at[spot, c], block_sem.at[0])
    block_out = remote(w_ref, wbuf.at[spot, c], block_sem.at[1], block_sem.at[2], partner)

    @pl.when(home == c)
    def _():
        block_local.start()

    @pl.when(home != c)
    def _():
        block_out.start()

    base = {A: (x, y * parts), D: (1 - x, (1 - y) * parts),
            X: (1 - x, y * parts), Y: (x, (1 - y) * parts)}

    def slot(i):
        s = jnp.where(z <= slots * c, i, slots - 1 - i)
        source = slots * c + s
        ends = (source == 0) | (source == nz - 1)
        return s, source, jnp.abs(source - z), ends

    def relay(s, what, j, lane, to_kind, device):
        rows, first = base[what]
        ref = wbuf.at[s, rows, first + j]
        return remote(ref, ref, rel_send.at[s, lane, j], w_recv.at[s, to_kind, j], device)

    def arrived(s, what, j):
        relay(s, what, j, 0, what, x_nb).wait_recv()

    def onward(source):
        to = jnp.where(source < z, z + 1, z - 1)
        return (to >= 0) & (to < nz), dev(z_=jnp.clip(to, 0, nz - 1))

    def relays_a(s, source, j):
        more, to = onward(source)
        return (
            (more, relay(s, A, j, 2, A, to)),
            (None, relay(s, A, j, 0, X, x_nb)),
            (None, relay(s, A, j, 1, Y, y_nb)),
        )

    def on_a(distance, j):
        for i in range(slots):
            s, source, far, ends = slot(i)

            @pl.when(far == distance)
            def _():
                arrived(s, A, j)
                for needed, copy in relays_a(s, source, j):
                    if needed is None:
                        copy.start()
                    else:
                        @pl.when(needed)
                        def _():
                            copy.start()

    def on_xy(wanted, j):
        for i in range(slots):
            s, source, far, ends = slot(i)
            by_x = jnp.where(far == 1, (2 * parts) // PIECES, parts // PIECES)

            @pl.when((far > 0) & wanted(far, ends))
            def _():
                arrived(s, X, j)
                arrived(s, Y, j)

                @pl.when(jnp.logical_not(ends) & (j < by_x))
                def _():
                    relay(s, Y, j, 3, D, x_nb).start()

                @pl.when(jnp.logical_not(ends) & (j >= by_x))
                def _():
                    relay(s, X, j, 3, D, y_nb).start()

    def on_d(i, wanted, j):
        s, source, far, ends = slot(i)

        @pl.when((far > 0) & wanted(far, ends))
        def _():
            arrived(s, D, j)
            more, to = onward(source)

            @pl.when(ends & more)
            def _():
                relay(s, D, j, 3, D, to).start()

    def on_block(i):
        s, source, far, ends = slot(i)

        @pl.when(far == 0)
        def _():
            block_local.wait()
            other = wbuf.at[spot, 1 - c]
            remote(w_ref, other, block_sem.at[1], block_sem.at[2], partner).wait_recv()

    def drain(i):
        s, source, far, ends = slot(i)
        more, to = onward(source)

        def one(j):
            for needed, copy in relays_a(s, source, j):
                if needed is None:
                    copy.wait_send()
                else:
                    @pl.when(needed)
                    def _():
                        copy.wait_send()

            @pl.when(jnp.logical_not(ends) | more)
            def _():
                relay(s, X, j, 3, D, y_nb).wait_send()

        @pl.when(far > 0)
        def _():
            each(parts, one)

    def rs(j):
        return remote(rs_send.at[j], rs_recv.at[j], rs_out.at[j], rs_in.at[j], x_nb)

    loads[0].wait()
    loads[1].wait()
    ones = jnp.ones((tokens, LANES), jnp.bfloat16)
    for j in range(half):
        for h in (j, half + j):
            cols = slice(h * HD, (h + 1) * HD)
            kp = jnp.maximum(k_ref[:, cols], 0)
            dims = (((0,), (0,)), ((), ()))
            st[h, :, :HD] = lax.dot_general(
                kp, v_ref[:, cols], dims, preferred_element_type=jnp.float32)
            total = lax.dot_general(kp, ones, dims, preferred_element_type=jnp.float32)
            st[h, :, HD:] = total[:, HD:]
        rs_send[j] = st[(1 - x) * half + j].astype(jnp.bfloat16)
        rs(j).start()
        on_a(1, j)

    def up(j):
        return remote(fin.at[x * half + j], z_recv.at[j], z_out.at[j], z_in.at[j],
                      dev(z_=jnp.minimum(z + 1, nz - 1)))

    def across(j):
        ref = fin.at[x * half + j]
        return remote(ref, ref, ag_out.at[j], ag_in.at[j], x_nb)

    def finish(j, total):
        fin[x * half + j] = total.astype(jnp.bfloat16)

        @pl.when(z < nz - 1)
        def _():
            up(j).start()
        across(j).start()

    @pl.when((c != x) & ((z == 0) | (z == nz - 1)))
    def _():
        own_each(lambda copy: copy.start())

    def near_step(j):
        rs(j).wait_recv()
        total = st[x * half + j] + rs_recv[j].astype(jnp.float32)
        own5[j] = total

        @pl.when(z == 0)
        def _():
            finish(j, total)

    def next_step(j):
        on_a(2, j)
        on_xy(lambda far, ends: (far == 1) & jnp.logical_not(ends), j)

        @pl.when(z > 0)
        def _():
            up(j).wait_recv()
            finish(j, own5[j] + z_recv[j].astype(jnp.float32))

    def far_step(j):
        on_a(3, j)
        for i in range(slots):
            on_d(i, lambda far, ends: (far == 1) & ends, j)
        on_xy(lambda far, ends: (far == 2) & jnp.logical_not(ends), j)

    def last_step(j):
        for i in range(slots):
            on_d(i, lambda far, ends: (far == 2) & ends, j)

    each(half, near_step)
    each(half, next_step)
    each(parts, far_step)
    each(parts, last_step)

    def across_in(j):
        ref = fin.at[(1 - x) * half + j]
        remote(ref, ref, ag_out.at[j], ag_in.at[j], x_nb).wait_recv()

    each(half, across_in)

    loads[2].wait()
    for h in range(heads):
        qp = jnp.maximum(q_ref[:, h * HD:(h + 1) * HD], 0)
        both = jnp.dot(qp, fin[h], preferred_element_type=jnp.float32)
        share = both[:, :HD] / (both[:, HD:HD + 1] + EPS)
        att[c, :, h * HD:(h + 1) * HD] = share.astype(jnp.bfloat16)
    att_out = remote(att.at[c], att.at[c], at_sem.at[0], at_sem.at[1], partner)
    att_out.start()
    each(parts, lambda j: on_xy(lambda far, ends: ends, j))
    remote(att.at[1 - c], att.at[1 - c], at_sem.at[0], at_sem.at[1], partner).wait_recv()

    for i in range(slots):
        s = slot(i)[0]
        on_block(i)
        each(parts, lambda j: on_d(
            i, lambda far, ends: (far > 2) | jnp.logical_not(ends), j))
        out = None
        for r in range(2):
            part = lax.dot_general(
                att[r], wbuf[s, r].reshape(wide, features),
                (((1,), (1,)), ((), ())), preferred_element_type=jnp.float32,
            )
            out = part if out is None else out + part
        out = out.astype(out_ref.dtype)
        for place in range(slots):
            @pl.when(s == place)
            def _():
                out_ref[:, place * wide:(place + 1) * wide] = out

    @pl.when((c == x) | (z == 0) | (z == nz - 1))
    def _():
        own_each(lambda copy: copy.wait_send())

    @pl.when(home != c)
    def _():
        block_out.wait_send()

    def sent(j):
        rs(j).wait_send()
        across(j).wait_send()

        @pl.when(z < nz - 1)
        def _():
            up(j).wait_send()

    each(half, sent)
    att_out.wait_send()
    for i in range(slots):
        drain(i)


def fused(nz, queries, keys, values, out_weight):
    frames_here, rows_here, columns, features = queries.shape
    tokens = frames_here * rows_here * columns
    heads, half, wide = features // HD, features // HD // 2, out_weight.shape[1]
    slots = nz // 2
    chunks = 2 * PIECES
    parts = PIECES
    width = wide // chunks
    vmem, hbm = pl.BlockSpec(memory_space=pltpu.VMEM), pl.BlockSpec(memory_space=pl.ANY)
    bf16, f32 = jnp.bfloat16, jnp.float32
    dma = pltpu.SemaphoreType.DMA
    out = pl.pallas_call(
        functools.partial(kernel, nz),
        out_shape=jax.ShapeDtypeStruct((tokens, slots * wide), bf16),
        in_specs=[hbm] * 4,
        out_specs=vmem,
        scratch_shapes=[
            pltpu.VMEM((tokens, features), bf16),
            pltpu.VMEM((tokens, features), bf16),
            pltpu.VMEM((tokens, features), bf16),
            pltpu.VMEM((slots, 2, chunks, width, features), bf16),
            pltpu.VMEM((2, tokens, features), bf16),
            pltpu.VMEM((heads, HD, LANES), f32),
            pltpu.VMEM((half, HD, LANES), f32),
            pltpu.VMEM((half, HD, LANES), bf16),
            pltpu.VMEM((half, HD, LANES), bf16),
            pltpu.VMEM((half, HD, LANES), bf16),
            pltpu.VMEM((heads, HD, LANES), bf16),
            dma((3,)),
            dma((slots, 4, parts)),
            dma((2, parts)),
            dma((slots, 4, parts)),
            dma((3,)),
            dma((half,)),
            dma((half,)),
            dma((half,)),
            dma((half,)),
            dma((half,)),
            dma((half,)),
            dma((2,)),
        ],
        compiler_params=pltpu.CompilerParams(
            collective_id=0, has_side_effects=True, vmem_limit_bytes=56 * 2**20),
        name="attend_project",
    )(
        queries.reshape(tokens, features),
        keys.reshape(tokens, features),
        values.reshape(tokens, features),
        out_weight.T.reshape(chunks, width, features),
    )
    return out.reshape(frames_here, rows_here, columns, slots * wide)


def solution(mesh):
    size = dict(mesh.shape)
    pairs = size["rows"] == 2 and size["groups"] == 2 and size["heads"] == 2
    body = general
    if pairs and size["frames"] == 4:
        body = functools.partial(fused, size["frames"])
    return jax.shard_map(
        body,
        mesh=mesh,
        in_specs=(
            P(("groups", "frames"), "rows", None, "heads"),
            P(("groups", "frames"), "rows", None, "heads"),
            P(("groups", "frames"), "rows", None, "heads"),
            P("heads", "frames"),
        ),
        out_specs=P(("groups", "frames"), "rows", None, "heads"),
        check_vma=False,
    )
```
